32 devices in a mesh: grp: 16 (over z, x, core), blk: 2 (over y).
Axes of the slice: x: 2, y: 2, z: 4, core: 2. Of those that a mesh axis runs over, the one named last changes fastest.
Arguments:
- walker_matrix: float32 [16, 2, 1024, 1024], P('grp', 'blk'), may hold values from -6 to 6
- updates: bfloat16 [16, 2, 4, 1024, 256], P('grp', 'blk'), may hold values from -0.19921875 to 0.19921875
- update_rows: int32 [16, 2, 4, 256], P('grp', 'blk'), may hold values from 0 to 1023, as said below
- left_table: float32 [1024, 256], replicated, may hold values from -0.1875 to 0.1875
- right_table: float32 [1024, 256], replicated, may hold values from -0.1875 to 0.1875
- assignment: int32 [2, 16], P('blk'), may hold values from 0 to 15, each once within a row
- momentum_sum: int32 [16, 16], replicated, may hold values from 0 to 15, as said below
- transfer_momentum: int32 [8], replicated, may hold values from 0 to 15
- transfer_frequency: int32 [8], replicated, may hold values from 0 to 15
- ownership: int32 [8], P('blk'), may hold values from 0 to 7, each once
- g4_prior: float32 [16, 8, 256, 256], P('grp', 'blk'), may hold values from -6 to 6
Outputs:
- g4_slices: float32 [16, 8, 256, 256], P('grp', 'blk')
The draws below stay inside these ranges and needn't reach their ends.
Inputs may be any that keep to these rules, and one draw needn't show every extreme that they name: `update_rows`: within each update of each walker the 256 row indices are distinct. `assignment`: each row is a permutation of the grp indices. `momentum_sum`: the addition table of a periodic 4 x 4 cluster under a relabeling of its momenta; every row and column is a permutation. `ownership`: a permutation of the transfer slots.
All inputs are finite; a program needn't handle non-finite values.
Results may differ from the reference program's by a relative error of at most 0.0003.
Values sent between devices are 32-bit elements; how exact they have to be, the bound alone decides.
A program may use at most 128 MiB of HBM per device.

```python
import jax
import jax.numpy as jnp
from jax import lax

ORDER = 1024
RANK = 256
UPD = 4
CL = 4
NW = 16
NK = 16
KW = 256
Q = 8
N_GRP = 16
N_BLK = 2


def draw_update_rows(key, part):
    keys = jax.random.split(jax.random.fold_in(key, 11), N_GRP * N_BLK * UPD)
    drawn = jax.vmap(lambda one_key: jax.random.permutation(one_key, ORDER)[:RANK])(keys)
    return drawn.reshape(N_GRP, N_BLK, UPD, RANK).astype(jnp.int32)


def draw_momentum_sum(key, part):
    relabel = jax.random.permutation(jax.random.fold_in(key, 17), NK).astype(jnp.int32)
    inverse = jnp.zeros((NK,), jnp.int32).at[relabel].set(jnp.arange(NK, dtype=jnp.int32))
    first = inverse[:, None]
    second = inverse[None, :]
    combined = (first // CL + second // CL) % CL * CL + (first % CL + second % CL) % CL
    return relabel[combined].astype(jnp.int32)


def with_ends(values, own_key, least, largest):
    longest = values.shape.index(max(values.shape))
    spots = []
    for shift in (0, 1):
        where = [jax.random.randint(jax.random.fold_in(own_key, axis), (), 0, length) for axis, length in enumerate(values.shape)]
        where[longest] = (where[longest] + shift) % values.shape[longest]
        spots.append(tuple(where))
    return values.at[spots[0]].set(least).at[spots[1]].set(largest)


def level_of(rng, dims, shards, smallest, largest):
    def one(dim, shards_of):
        heights = jax.random.uniform(jax.random.fold_in(jax.random.fold_in(rng, 6), dim), (shards_of,), jnp.float32, smallest / len(shards), largest / len(shards))
        return jnp.repeat(jnp.exp(heights), dims[dim] // shards_of).reshape((-1,) + (1,) * (len(dims) - dim - 1))

    loudness = one(*shards[0])
    for cut in shards[1:]:
        loudness = loudness * one(*cut)
    return loudness


def noise(key, dims, scale, bound, cuts=(), kind=jnp.bfloat16):
    loudness = level_of(key, dims, cuts, -0.22, 0.18) if cuts else 1.0
    entries = jax.random.normal(key, dims, jnp.float32) * scale * loudness
    return jnp.minimum(jnp.maximum(entries, -bound), bound).astype(kind)


def setup_inputs(seed: int = 0) -> dict:
    arg_keys = jax.random.split(jax.random.key(seed), 12)
    return {
        "walker_matrix": noise(arg_keys[0], (N_GRP, N_BLK, ORDER, ORDER), 1.0, 6.0, ((0, 16), (1, 2)), jnp.float32),
        "updates": noise(arg_keys[1], (N_GRP, N_BLK, UPD, ORDER, RANK), 0.03125, 0.19921875, ((0, 16), (1, 2))),
        "update_rows": draw_update_rows(jax.random.fold_in(arg_keys[11], 71), 0),
        "left_table": noise(arg_keys[3], (ORDER, KW), ORDER ** -0.5, 0.1875, (), jnp.float32),
        "right_table": noise(arg_keys[4], (ORDER, KW), ORDER ** -0.5, 0.1875, (), jnp.float32),
        "assignment": jax.vmap(lambda own: jax.random.permutation(own, N_GRP))(jax.random.split(arg_keys[5], N_BLK)).reshape((N_BLK, N_GRP)).astype(jnp.int32),
        "momentum_sum": draw_momentum_sum(jax.random.fold_in(arg_keys[11], 71), 0),
        "transfer_momentum": with_ends(jax.random.randint(arg_keys[7], (Q,), 0, NK), jax.random.fold_in(arg_keys[7], 1), 0, NK - 1).astype(jnp.int32),
        "transfer_frequency": with_ends(jax.random.randint(arg_keys[8], (Q,), 0, NW), jax.random.fold_in(arg_keys[8], 1), 0, NW - 1).astype(jnp.int32),
        "ownership": jax.random.permutation(arg_keys[9], Q).astype(jnp.int32),
        "g4_prior": noise(arg_keys[10], (N_GRP, Q, KW, KW), 1.0, 6.0, ((0, 16), (1, 2)), jnp.float32),
    }


highest = lax.Precision.HIGHEST


def measure_walker(matrix, updates_here, rows_here, left_table, right_table):
    for number in range(UPD):
        picked = matrix[rows_here[number]]
        matrix = matrix + jnp.dot(updates_here[number].astype(jnp.float32), picked, precision=highest)
    partial_value = jnp.dot(matrix, right_table, precision=highest)
    return jnp.dot(left_table.T, partial_value, precision=highest)


def shift_rows(momentum_sum, moment_ids, freq_ids):
    labels = jnp.arange(KW, dtype=jnp.int32)
    momenta = labels // NW
    frequency = labels % NW
    return momentum_sum[momenta[None, :], moment_ids[:, None]] * NW + (frequency[None, :] + freq_ids[:, None]) % NW


def cycle_terms(greens_cycle, shifted):
    flipped = jnp.swapaxes(greens_cycle, 1, 2)

    def one_transfer(row_ids):
        picked = jnp.take(flipped, row_ids, axis=1)
        picked = jnp.take(picked, row_ids, axis=2)
        return jnp.sum(greens_cycle * picked, axis=0)

    return jax.vmap(one_transfer)(shifted)


def reference(walker_matrix, updates, update_rows, left_table, right_table, assignment, momentum_sum, transfer_momentum, transfer_frequency, ownership, g4_prior):
    walkers = N_GRP * N_BLK
    greens = lax.map(lambda walker_items: measure_walker(walker_items[0], walker_items[1], walker_items[2], left_table, right_table),
                     (walker_matrix.reshape(walkers, ORDER, ORDER), updates.reshape(walkers, UPD, ORDER, RANK), update_rows.reshape(walkers, UPD, RANK)))
    greens = greens.reshape(N_GRP, N_BLK, KW, KW)
    chosen = (assignment[:, :, None] == jnp.arange(N_GRP, dtype=jnp.int32)[None, None, :]).astype(jnp.float32)
    measured = jnp.einsum("bwa,wbij->abij", chosen, greens, precision=highest)
    shifted = shift_rows(momentum_sum, transfer_momentum[ownership], transfer_frequency[ownership])
    summed = lax.map(lambda cycle_greens: cycle_terms(cycle_greens, shifted), measured)
    return g4_prior + summed * (1.0 / N_BLK)
```

```python
import functools

import jax
import jax.numpy as jnp
from jax import lax
from jax.experimental import pallas as pl
from jax.experimental.pallas import tpu as pltpu
from jax.sharding import PartitionSpec as P

MESH = pl.DeviceIdType.MESH
F32 = jnp.float32
BF16 = jnp.bfloat16


def split(x):
    hi = x.astype(BF16)
    return hi, (x - hi.astype(F32)).astype(BF16)


def nn(a, b):
    return jnp.dot(a, b, preferred_element_type=F32)


def nt(a, b):
    return lax.dot_general(a, b, (((1,), (1,)), ((), ())), preferred_element_type=F32)


def exchange_kernel(
    groups, blocks, target_ref, own_ref, mom_ref, freq_ref, sum_ref, m_hbm, u_hbm, rows_hbm, l_hbm, r_hbm, prior_hbm, out_ref,
    m_v, u_v, rows_v, l_v, r_v, pick_v, zh_v, zl_v, g_v, arranged, seen, perm_v, source,
    sems, s1, r1, s2, r2, s3, r3, *spread,
):
    grp = lax.axis_index("grp")
    blk = lax.axis_index("blk")
    number, order, rank = u_v.shape
    halves, cols, _, rows, width = g_v.shape
    kw = cols * width
    kh = kw // halves
    parts = 4
    step = order // parts
    slots = out_ref.shape[0]
    chunks = [(h, c) for h in range(halves) for c in range(cols)]
    pairs = list(range(1, groups))

    def partner(i):
        place, bit = grp, 1
        while bit <= i:
            if i & bit:
                place = place + bit - 2 * bit * lax.rem(grp // bit, 2)
            bit *= 2
        return place

    def group_peer(i):
        return {"grp": partner(i), "blk": blk}

    def block_peer(i):
        return {"grp": grp, "blk": lax.rem(blk + i, blocks)}

    copy_rows = pltpu.make_async_copy(rows_hbm, rows_v, sems.at[0])
    copy_l = pltpu.make_async_copy(l_hbm, l_v, sems.at[1])
    copy_r = pltpu.make_async_copy(r_hbm, r_v, sems.at[2])
    copy_p = pltpu.make_async_copy(prior_hbm, out_ref, sems.at[3])
    copy_u = [pltpu.make_async_copy(u_hbm.at[i], u_v.at[i], sems.at[4 + i]) for i in range(number)]
    copy_m = [
        pltpu.make_async_copy(m_hbm.at[pl.ds(i * step, step)], m_v.at[pl.ds(i * step, step)], sems.at[4 + number + i])
        for i in range(parts)
    ]
    copy_rows.start()
    copy_l.start()
    for i in reversed(range(number)):
        copy_u[i].start()
    copy_r.start()
    for c in copy_m:
        c.start()
    copy_p.start()

    barrier = pltpu.get_barrier_semaphore()

    for i in pairs:
        pl.semaphore_signal(barrier, inc=1, device_id=group_peer(i), device_id_type=MESH)

    @pl.loop(1, blocks)
    def _(i):
        pl.semaphore_signal(barrier, inc=1, device_id=block_peer(i), device_id_type=MESH)

    targets = [target_ref[0, w] for w in range(groups)]
    for a in range(groups):
        found = 0
        for w in range(groups):
            found = jnp.where(targets[w] == a, w, found)
        source[a] = found

    copy_rows.wait()
    for i in reversed(range(number)):
        pick_v[i] = jnp.where(
            lax.broadcasted_iota(jnp.int32, (order, rank), 0) == rows_v[pl.ds(i, 1), :], 1.0, 0.0
        ).astype(BF16)

    momenta = sum_ref.shape[0]
    nw = kw // momenta
    sub = lax.broadcasted_iota(jnp.int32, (nw, kw), 0)
    lane = lax.broadcasted_iota(jnp.int32, (nw, kw), 1)
    for j in range(slots):
        t = own_ref[j]
        q = mom_ref[t]
        moved = sub + freq_ref[t]
        base = lane - jnp.where(moved >= nw, moved - nw, moved)
        for kappa in range(momenta):
            hit = jnp.where(base == sum_ref[kappa, q] * nw, 1.0, 0.0).astype(BF16)
            perm_v[j * kw + kappa * nw:j * kw + (kappa + 1) * nw, :] = hit

    def accumulate(b):
        g = jnp.concatenate(
            [jnp.concatenate([seen[b, h, c].reshape(kh, width) for c in range(cols)], axis=1) for h in range(halves)],
            axis=0)
        gh, gl = split(g)
        xh = nt(perm_v[...], gh).astype(BF16)
        xl = nt(perm_v[...], gl).astype(BF16)
        for j in range(slots):
            rows_j = slice(j * kw, (j + 1) * kw)
            y = nt(jnp.concatenate([xh[rows_j], xl[rows_j]], axis=0), perm_v[rows_j, :])
            term = g * (y[:kw] + y[kw:])
            out_ref[j] = out_ref[j] + term * (1.0 / blocks)

    def chain(h):
        w = jnp.transpose(l_v[:, h * kh:(h + 1) * kh])
        for i in reversed(range(number)):
            if h == 0:
                copy_u[i].wait()
            t = nn(jnp.concatenate(split(w), axis=0), u_v[i])
            t = nt(jnp.concatenate(split(t[:kh] + t[kh:]), axis=0), pick_v[i])
            w = w + (t[:kh] + t[kh:])
        return split(w)

    def finish(h, wh, wl):
        t = nn(jnp.concatenate([wh, wl], axis=0), zh_v[...])
        g = t[:kh] + t[kh:] + nn(wh, zl_v[...])
        for c in range(cols):
            g_v[h, c] = g[:, c * width:(c + 1) * width].reshape(groups, rows, width)

    def first(k, i):
        h, c = chunks[k]
        return pltpu.make_async_remote_copy(
            g_v.at[h, c, partner(i)], spread[k].at[grp], s1.at[0], r1.at[k],
            device_id=group_peer(i), device_id_type=MESH)

    def second(k, i):
        h, c = chunks[k]
        return pltpu.make_async_remote_copy(
            arranged.at[h, c, partner(i)], seen.at[blk, h, c, grp], s2.at[0], r2.at[k],
            device_id=group_peer(i), device_id_type=MESH)

    def third(k, i):
        h, c = chunks[k]
        return pltpu.make_async_remote_copy(
            seen.at[blk, h, c], seen.at[blk, h, c], s3.at[0], r3.at[i],
            device_id=block_peer(i), device_id_type=MESH)

    def pieces(k, recv, send):
        h, c = chunks[k]
        return pltpu.make_async_remote_copy(
            arranged.at[h, c, pl.ds(0, groups - 1)], spread[k].at[pl.ds(0, groups - 1)], send, recv,
            device_id=block_peer(1), device_id_type=MESH)

    def whole(recv, send):
        return pltpu.make_async_remote_copy(
            seen.at[blk], seen.at[blk], send, recv, device_id=block_peer(1), device_id_type=MESH)

    copy_l.wait()
    wh, wl = chain(0)
    copy_r.wait()
    rh, rl = split(r_v[...])
    for i in range(parts):
        copy_m[i].wait()
        mh, ml = split(m_v[pl.ds(i * step, step), :])
        t = nn(jnp.concatenate([mh, ml], axis=0), rh)
        zh, zl = split(t[:step] + t[step:] + nn(mh, rl))
        zh_v[pl.ds(i * step, step), :] = zh
        zl_v[pl.ds(i * step, step), :] = zl
    finish(0, wh, wl)

    pl.semaphore_wait(barrier, groups + blocks - 2)

    for k, (h, c) in enumerate(chunks):
        if h > 0 and c == 0:
            finish(h, *chain(h))
        for i in pairs:
            first(k, i).start()
        spread[k][grp] = g_v[h, c, grp]

    for k, (h, c) in enumerate(chunks):
        pieces(k, r1.at[k], s1.at[0]).wait_recv()
        for i in pairs:
            a = partner(i)
            arranged[h, c, a] = spread[k][source[a]]
            second(k, i).start()
        seen[blk, h, c, grp] = spread[k][source[grp]]

    for k in range(len(chunks)):
        pieces(k, r2.at[k], s2.at[0]).wait_recv()
        for i in range(1, blocks):
            third(k, i).start()

    copy_p.wait()
    accumulate(blk)

    for i in range(1, blocks):
        whole(r3.at[i], s3.at[0]).wait_recv()
        accumulate(lax.rem(blk + blocks - i, blocks))

    for k in range(len(chunks)):
        pieces(k, r1.at[k], s1.at[0]).wait_send()
        pieces(k, r2.at[k], s2.at[0]).wait_send()
    for i in range(1, blocks):
        whole(r3.at[i], s3.at[0]).wait_send()


def shards(
    walker_matrix,
    updates,
    update_rows,
    left_table,
    right_table,
    assignment,
    momentum_sum,
    transfer_momentum,
    transfer_frequency,
    ownership,
    g4_prior,
):
    groups = lax.axis_size("grp")
    blocks = lax.axis_size("blk")
    order, kw = left_table.shape
    number, rank = updates.shape[2], updates.shape[4]
    smem = pl.BlockSpec(memory_space=pltpu.SMEM)
    hbm = pl.BlockSpec(memory_space=pltpu.HBM)
    halves = 2 if kw // groups % 16 == 0 else 1
    cols = 2 if kw % 256 == 0 else 1
    rows, width = kw // groups // halves, kw // cols
    slots = g4_prior.shape[1]
    room = 4 * slots * kw * kw
    summed = pl.pallas_call(
        functools.partial(exchange_kernel, groups, blocks),
        out_shape=pltpu.VMEM((slots, kw, kw), F32),
        in_specs=[smem] * 5 + [hbm] * 6,
        out_specs=pl.BlockSpec(memory_space=pltpu.VMEM),
        scratch_shapes=[
            pltpu.VMEM((order, order), F32),
            pltpu.VMEM((number, order, rank), BF16),
            pltpu.VMEM((number, rank), jnp.int32),
            pltpu.VMEM((order, kw), F32),
            pltpu.VMEM((order, kw), F32),
            pltpu.VMEM((number, order, rank), BF16),
            pltpu.VMEM((order, kw), BF16),
            pltpu.VMEM((order, kw), BF16),
            pltpu.VMEM((halves, cols, groups, rows, width), F32),
            pltpu.VMEM((halves, cols, groups, rows, width), F32),
            pltpu.VMEM((blocks, halves, cols, groups, rows, width), F32),
            pltpu.VMEM((slots * kw, kw), BF16),
            pltpu.SMEM((groups,), jnp.int32),
            pltpu.SemaphoreType.DMA((number + 8,)),
            pltpu.SemaphoreType.DMA((1,)),
            pltpu.SemaphoreType.DMA((halves * cols,)),
            pltpu.SemaphoreType.DMA((1,)),
            pltpu.SemaphoreType.DMA((halves * cols,)),
            pltpu.SemaphoreType.DMA((1,)),
            pltpu.SemaphoreType.DMA((blocks,)),
        ] + [pltpu.VMEM((groups, rows, width), F32)] * (halves * cols),
        compiler_params=pltpu.CompilerParams(
            collective_id=0, has_side_effects=True, vmem_limit_bytes=67043328 - room),
        name="exchange",
    )(assignment, ownership, transfer_momentum, transfer_frequency, momentum_sum,
      walker_matrix[0, 0], updates[0, 0], update_rows[0, 0], left_table, right_table, g4_prior[0])
    return summed[None]


def solution(mesh):
    placed = (
        P("grp", "blk", None, None),
        P("grp", "blk", None, None, None),
        P("grp", "blk", None, None),
        P(),
        P(),
        P("blk", None),
        P(),
        P(),
        P(),
        P("blk"),
        P("grp", "blk", None, None),
    )
    return jax.shard_map(
        shards, mesh=mesh, in_specs=placed, out_specs=P("grp", "blk", None, None), check_vma=False
    )
```

```python
import functools

import jax
import jax.numpy as jnp
from jax import lax
from jax.experimental import pallas as pl
from jax.experimental.pallas import tpu as pltpu
from jax.sharding import PartitionSpec as P

MESH = pl.DeviceIdType.MESH
F32 = jnp.float32
BF16 = jnp.bfloat16


def split(x):
    hi = x.astype(BF16)
    return hi, (x - hi.astype(F32)).astype(BF16)


def nn(a, b):
    return jnp.dot(a, b, preferred_element_type=F32)


def nt(a, b):
    return lax.dot_general(a, b, (((1,), (1,)), ((), ())), preferred_element_type=F32)


def exchange_kernel(
    groups, blocks, target_hbm, own_hbm, mom_hbm, freq_hbm, sum_hbm, m_hbm, u_hbm, rows_hbm, l_hbm, r_hbm, prior_hbm, out_ref,
    target_ref, own_ref, mom_ref, freq_ref, sum_ref, m_v, u_v, rows_v, l_v, r_v, pick_v, rh_v, rl_v, zh_v, zl_v, g_v, arranged, seen, perm_v, part_v, source,
    sems, s1, r1, s2, r2, s3, r3, s4, r4, *spread,
):
    grp = lax.axis_index("grp")
    blk = lax.axis_index("blk")
    number, order, rank = u_v.shape
    halves, cols, _, rows, width = g_v.shape
    kw = cols * width
    kh = kw // halves
    parts = 4
    step = order // parts
    slots = out_ref.shape[0]
    chunks = [(h, c) for h in range(halves) for c in range(cols)]
    pairs = list(range(1, groups))

    def partner(i):
        place, bit = grp, 1
        while bit <= i:
            if i & bit:
                place = place + bit - 2 * bit * lax.rem(grp // bit, 2)
            bit *= 2
        return place

    def group_peer(i):
        return {"grp": partner(i), "blk": blk}

    def block_peer(i):
        return {"grp": grp, "blk": lax.rem(blk + i, blocks)}

    copy_rows = pltpu.make_async_copy(rows_hbm, rows_v, sems.at[0])
    copy_l = pltpu.make_async_copy(l_hbm, l_v, sems.at[1])
    copy_r = pltpu.make_async_copy(r_hbm, r_v, sems.at[2])
    copy_p = pltpu.make_async_copy(prior_hbm, out_ref, sems.at[3])
    copy_u = [pltpu.make_async_copy(u_hbm.at[i], u_v.at[i], sems.at[4 + i]) for i in range(number)]
    copy_m = [
        pltpu.make_async_copy(m_hbm.at[pl.ds(i * step, step)], m_v.at[pl.ds(i * step, step)], sems.at[4 + number + i])
        for i in range(parts)
    ]
    copy_rows.start()
    copy_l.start()
    copy_u[number - 1].start()
    copy_r.start()
    copy_m[0].start()

    small = [(target_hbm, target_ref), (own_hbm, own_ref), (mom_hbm, mom_ref), (freq_hbm, freq_ref), (sum_hbm, sum_ref)]
    small = [pltpu.make_async_copy(a, b, sems.at[4 + number + parts + i]) for i, (a, b) in enumerate(small)]
    for c in small:
        c.start()

    barrier = pltpu.get_barrier_semaphore()

    for i in pairs:
        pl.semaphore_signal(barrier, inc=1, device_id=group_peer(i), device_id_type=MESH)

    @pl.loop(1, blocks)
    def _(i):
        pl.semaphore_signal(barrier, inc=1, device_id=block_peer(i), device_id_type=MESH)

    copy_rows.wait()
    for i in reversed(range(number)):
        pick_v[i] = jnp.where(
            lax.broadcasted_iota(jnp.int32, (order, rank), 0) == rows_v[pl.ds(i, 1), :], 1.0, 0.0
        ).astype(BF16)

    def rows_of(b, h):
        return jnp.concatenate([seen[b, h, c].reshape(kh, width) for c in range(cols)], axis=1)

    def accumulate(b, h):
        x = nt(perm_v[...], jnp.concatenate(split(rows_of(b, h)), axis=0)).astype(BF16)
        last = h == halves - 1
        if last:
            g = jnp.concatenate([rows_of(b, i) for i in range(halves)], axis=0)
        for j in range(slots):
            here = slice(j * kw, (j + 1) * kw)
            p = perm_v[here, h * kh:(h + 1) * kh]
            y = nt(x[here], jnp.concatenate([p, p], axis=1))
            if h > 0:
                y = y + part_v[b, j]
            if last:
                out_ref[j] = out_ref[j] + g * y * (1.0 / blocks)
            else:
                part_v[b, j] = y

    def apply(h, w, i, between=None):
        t = nn(jnp.concatenate(split(w), axis=0), u_v[i])
        if between:
            between()
        t = nt(jnp.concatenate(split(t[:kh] + t[kh:]), axis=0), pick_v[i])
        return w + (t[:kh] + t[kh:])

    def project(i):
        mh, ml = split(m_v[pl.ds(i * step, step), :])
        t = nn(jnp.concatenate([mh, ml], axis=0), rh_v[...])
        zh, zl = split(t[:step] + t[step:] + nn(mh, rl_v[...]))
        zh_v[pl.ds(i * step, step), :] = zh
        zl_v[pl.ds(i * step, step), :] = zl

    def finish(h, wh, wl):
        t = nn(jnp.concatenate([wh, wl], axis=0), zh_v[...])
        g = t[:kh] + t[kh:] + nn(wh, zl_v[...])
        for c in range(cols):
            g_v[h, c] = g[:, c * width:(c + 1) * width].reshape(groups, rows, width)

    def first(k, i):
        h, c = chunks[k]
        return pltpu.make_async_remote_copy(
            g_v.at[h, c, partner(i)], spread[k].at[grp], s1.at[0], r1.at[k],
            device_id=group_peer(i), device_id_type=MESH)

    def second(k, i):
        h, c = chunks[k]
        return pltpu.make_async_remote_copy(
            arranged.at[h, c, partner(i)], seen.at[blk, h, c, grp], s2.at[0], r2.at[k],
            device_id=group_peer(i), device_id_type=MESH)

    def third(k, i):
        h, c = chunks[k]
        return pltpu.make_async_remote_copy(
            seen.at[blk, h, c], seen.at[blk, h, c], s3.at[0], r3.at[i],
            device_id=block_peer(i), device_id_type=MESH)

    def across(c, i, j):
        return pltpu.make_async_remote_copy(
            arranged.at[halves - 1, c, partner(i)], seen.at[blk, halves - 1, c, grp], s4.at[0], r4.at[j, c],
            device_id={"grp": partner(i), "blk": lax.rem(blk + j, blocks)}, device_id_type=MESH)

    def pieces(k, recv, send):
        h, c = chunks[k]
        return pltpu.make_async_remote_copy(
            arranged.at[h, c, pl.ds(0, groups - 1)], spread[k].at[pl.ds(0, groups - 1)], send, recv,
            device_id=block_peer(1), device_id_type=MESH)

    def quarter(c, recv, send):
        return pltpu.make_async_remote_copy(
            arranged.at[halves - 1, c], seen.at[blk, halves - 1, c], send, recv, device_id=block_peer(1), device_id_type=MESH)

    def early(recv, send):
        return pltpu.make_async_remote_copy(
            seen.at[blk, pl.ds(0, halves - 1)], seen.at[blk, pl.ds(0, halves - 1)], send, recv,
            device_id=block_peer(1), device_id_type=MESH)

    copy_l.wait()
    copy_u[number - 1].wait()
    later = [copy_u[number - 2], copy_m[1], copy_u[number - 3], copy_m[2], copy_u[number - 4], copy_m[3], copy_p]
    for c in later[:4]:
        c.start()
    w = apply(0, jnp.transpose(l_v[:, :kh]), number - 1)
    copy_r.wait()
    rh_v[...], rl_v[...] = split(r_v[...])
    for i in range(parts):
        for c in later[4 + 2 * i:4 + 2 * i + 2]:
            c.start()
        copy_m[i].wait()
        u = number - 2 - i
        if u >= 0:
            copy_u[u].wait()
            w = apply(0, w, u, functools.partial(project, i))
        else:
            project(i)
    finish(0, *split(w))

    pl.semaphore_wait(barrier, groups + blocks - 2)

    for k, (h, c) in enumerate(chunks):
        if h > 0 and c == 0:
            w = jnp.transpose(l_v[:, h * kh:(h + 1) * kh])
            for i in reversed(range(number)):
                w = apply(h, w, i)
            finish(h, *split(w))
        for i in pairs:
            first(k, i).start()
        spread[k][grp] = g_v[h, c, grp]

    for c in small:
        c.wait()
    targets = [target_ref[0, w] for w in range(groups)]
    for a in range(groups):
        found = 0
        for w in range(groups):
            found = jnp.where(targets[w] == a, w, found)
        source[a] = found

    momenta = sum_ref.shape[0]
    nw = kw // momenta
    sub = lax.broadcasted_iota(jnp.int32, (nw, kw), 0)
    lane = lax.broadcasted_iota(jnp.int32, (nw, kw), 1)
    for j in range(slots):
        t = own_ref[j]
        q = mom_ref[t]
        moved = sub + freq_ref[t]
        base = lane - jnp.where(moved >= nw, moved - nw, moved)
        for kappa in range(momenta):
            hit = jnp.where(base == sum_ref[kappa, q] * nw, 1.0, 0.0).astype(BF16)
            perm_v[j * kw + kappa * nw:j * kw + (kappa + 1) * nw, :] = hit

    for k, (h, c) in enumerate(chunks):
        pieces(k, r1.at[k], s1.at[0]).wait_recv()
        for i in pairs:
            a = partner(i)
            arranged[h, c, a] = spread[k][source[a]]
            if h == halves - 1:
                for j in range(1, blocks):
                    across(c, i, j).start()
            second(k, i).start()
        mine = spread[k][source[grp]]
        seen[blk, h, c, grp] = mine
        if h == halves - 1:
            arranged[h, c, grp] = mine
            for j in range(1, blocks):
                across(c, 0, j).start()

    for k, (h, c) in enumerate(chunks):
        if h < halves - 1:
            pieces(k, r2.at[k], s2.at[0]).wait_recv()
            for j in range(1, blocks):
                third(k, j).start()

    def other(j):
        return lax.rem(blk + blocks - j, blocks)

    if halves > 1:
        for h in range(halves - 1):
            accumulate(blk, h)
        for j in range(1, blocks):
            early(r3.at[j], s3.at[0]).wait_recv()
            for h in range(halves - 1):
                accumulate(other(j), h)

    copy_p.wait()
    for k, (h, c) in enumerate(chunks):
        if h == halves - 1:
            pieces(k, r2.at[k], s2.at[0]).wait_recv()
    accumulate(blk, halves - 1)
    for j in range(1, blocks):
        for c in range(cols):
            quarter(c, r4.at[j, c], s4.at[0]).wait_recv()
        accumulate(other(j), halves - 1)

    for k in range(len(chunks)):
        pieces(k, r1.at[k], s1.at[0]).wait_send()
        pieces(k, r2.at[k], s2.at[0]).wait_send()
    for j in range(1, blocks):
        if halves > 1:
            early(r3.at[j], s3.at[0]).wait_send()
        for c in range(cols):
            quarter(c, r4.at[j, c], s4.at[0]).wait_send()


def shards(
    walker_matrix,
    updates,
    update_rows,
    left_table,
    right_table,
    assignment,
    momentum_sum,
    transfer_momentum,
    transfer_frequency,
    ownership,
    g4_prior,
):
    groups = lax.axis_size("grp")
    blocks = lax.axis_size("blk")
    order, kw = left_table.shape
    number, rank = updates.shape[2], updates.shape[4]
    hbm = pl.BlockSpec(memory_space=pltpu.HBM)
    halves = 2 if kw // groups % 16 == 0 else 1
    cols = 2 if kw % 256 == 0 else 1
    rows, width = kw // groups // halves, kw // cols
    slots = g4_prior.shape[1]
    room = 4 * slots * kw * kw
    summed = pl.pallas_call(
        functools.partial(exchange_kernel, groups, blocks),
        out_shape=pltpu.VMEM((slots, kw, kw), F32),
        in_specs=[hbm] * 11,
        out_specs=pl.BlockSpec(memory_space=pltpu.VMEM),
        scratch_shapes=[
            pltpu.SMEM(assignment.shape, jnp.int32),
            pltpu.SMEM(ownership.shape, jnp.int32),
            pltpu.SMEM(transfer_momentum.shape, jnp.int32),
            pltpu.SMEM(transfer_frequency.shape, jnp.int32),
            pltpu.SMEM(momentum_sum.shape, jnp.int32),
            pltpu.VMEM((order, order), F32),
            pltpu.VMEM((number, order, rank), BF16),
            pltpu.VMEM((number, rank), jnp.int32),
            pltpu.VMEM((order, kw), F32),
            pltpu.VMEM((order, kw), F32),
            pltpu.VMEM((number, order, rank), BF16),
            pltpu.VMEM((order, kw), BF16),
            pltpu.VMEM((order, kw), BF16),
            pltpu.VMEM((order, kw), BF16),
            pltpu.VMEM((order, kw), BF16),
            pltpu.VMEM((halves, cols, groups, rows, width), F32),
            pltpu.VMEM((halves, cols, groups, rows, width), F32),
            pltpu.VMEM((blocks, halves, cols, groups, rows, width), F32),
            pltpu.VMEM((slots * kw, kw), BF16),
            pltpu.VMEM((blocks, slots, kw, kw), F32),
            pltpu.SMEM((groups,), jnp.int32),
            pltpu.SemaphoreType.DMA((number + 13,)),
            pltpu.SemaphoreType.DMA((1,)),
            pltpu.SemaphoreType.DMA((halves * cols,)),
            pltpu.SemaphoreType.DMA((1,)),
            pltpu.SemaphoreType.DMA((halves * cols,)),
            pltpu.SemaphoreType.DMA((1,)),
            pltpu.SemaphoreType.DMA((blocks,)),
            pltpu.SemaphoreType.DMA((1,)),
            pltpu.SemaphoreType.DMA((blocks, cols)),
        ] + [pltpu.VMEM((groups, rows, width), F32)] * (halves * cols),
        compiler_params=pltpu.CompilerParams(
            collective_id=0, has_side_effects=True, vmem_limit_bytes=67043328 - room),
        name="exchange",
    )(assignment, ownership, transfer_momentum, transfer_frequency, momentum_sum,
      walker_matrix[0, 0], updates[0, 0], update_rows[0, 0], left_table, right_table, g4_prior[0])
    return summed[None]


def solution(mesh):
    placed = (
        P("grp", "blk", None, None),
        P("grp", "blk", None, None, None),
        P("grp", "blk", None, None),
        P(),
        P(),
        P("blk", None),
        P(),
        P(),
        P(),
        P("blk"),
        P("grp", "blk", None, None),
    )
    return jax.shard_map(
        shards, mesh=mesh, in_specs=placed, out_specs=P("grp", "blk", None, None), check_vma=False
    )
```

```python
import functools

import jax
import jax.numpy as jnp
from jax import lax
from jax.experimental import pallas as pl
from jax.experimental.pallas import tpu as pltpu
from jax.sharding import PartitionSpec as P

MESH = pl.DeviceIdType.MESH
F32 = jnp.float32
BF16 = jnp.bfloat16


def split(x):
    hi = x.astype(BF16)
    return hi, (x - hi.astype(F32)).astype(BF16)


def nn(a, b):
    return jnp.dot(a, b, preferred_element_type=F32)


def nt(a, b):
    return lax.dot_general(a, b, (((1,), (1,)), ((), ())), preferred_element_type=F32)


def exchange_kernel(
    groups, blocks, target_hbm, own_hbm, mom_hbm, freq_hbm, sum_hbm, m_hbm, u_hbm, rows_hbm, l_hbm, r_hbm, prior_hbm, out_ref,
    target_ref, own_ref, mom_ref, freq_ref, sum_ref, m_v, u_v, rows_v, l_v, r_v, pick_v, rh_v, rl_v, zh_v, zl_v, g_v, arranged, seen, perm_v, part_v, source,
    sems, s1, r1, s2, r2, s3, r3, *spread,
):
    grp = lax.axis_index("grp")
    blk = lax.axis_index("blk")
    number, order, rank = u_v.shape
    halves, cols, _, rows, width = g_v.shape
    kw = cols * width
    kh = kw // halves
    parts = 4
    step = order // parts
    slots = out_ref.shape[0]
    chunks = [(h, c) for h in range(halves) for c in range(cols)]
    pairs = list(range(1, groups))

    def partner(i):
        place, bit = grp, 1
        while bit <= i:
            if i & bit:
                place = place + bit - 2 * bit * lax.rem(grp // bit, 2)
            bit *= 2
        return place

    def group_peer(i):
        return {"grp": partner(i), "blk": blk}

    def block_peer(i):
        return {"grp": grp, "blk": lax.rem(blk + i, blocks)}

    copy_rows = pltpu.make_async_copy(rows_hbm, rows_v, sems.at[0])
    copy_l = pltpu.make_async_copy(l_hbm, l_v, sems.at[1])
    copy_r = pltpu.make_async_copy(r_hbm, r_v, sems.at[2])
    copy_p = pltpu.make_async_copy(prior_hbm, out_ref, sems.at[3])
    copy_u = [pltpu.make_async_copy(u_hbm.at[i], u_v.at[i], sems.at[4 + i]) for i in range(number)]
    copy_m = [
        pltpu.make_async_copy(m_hbm.at[pl.ds(i * step, step)], m_v.at[pl.ds(i * step, step)], sems.at[4 + number + i])
        for i in range(parts)
    ]
    copy_rows.start()
    copy_l.start()
    copy_u[number - 1].start()
    copy_r.start()
    copy_m[0].start()
    later = [copy_u[number - 2], copy_m[1], copy_u[number - 3], copy_m[2], copy_u[number - 4], copy_m[3], copy_p]
    for c in later:
        c.start()

    small = [(target_hbm, target_ref), (own_hbm, own_ref), (mom_hbm, mom_ref), (freq_hbm, freq_ref), (sum_hbm, sum_ref)]
    small = [pltpu.make_async_copy(a, b, sems.at[4 + number + parts + i]) for i, (a, b) in enumerate(small)]
    for c in small:
        c.start()

    barrier = pltpu.get_barrier_semaphore()

    for i in pairs:
        pl.semaphore_signal(barrier, inc=1, device_id=group_peer(i), device_id_type=MESH)

    @pl.loop(1, blocks)
    def _(i):
        pl.semaphore_signal(barrier, inc=1, device_id=block_peer(i), device_id_type=MESH)

    copy_rows.wait()
    for i in reversed(range(number)):
        pick_v[i] = jnp.where(
            lax.broadcasted_iota(jnp.int32, (order, rank), 0) == rows_v[pl.ds(i, 1), :], 1.0, 0.0
        ).astype(BF16)

    def rows_of(b, h):
        return jnp.concatenate([seen[b, h, c].reshape(kh, width) for c in range(cols)], axis=1)

    def accumulate(b, h):
        x = nt(perm_v[...], jnp.concatenate(split(rows_of(b, h)), axis=0)).astype(BF16)
        last = h == halves - 1
        if last:
            g = jnp.concatenate([rows_of(b, i) for i in range(halves)], axis=0)
        for j in range(slots):
            here = slice(j * kw, (j + 1) * kw)
            p = perm_v[here, h * kh:(h + 1) * kh]
            y = nt(x[here], jnp.concatenate([p, p], axis=1))
            if h > 0:
                y = y + part_v[b, j]
            if last:
                out_ref[j] = out_ref[j] + g * y * (1.0 / blocks)
            else:
                part_v[b, j] = y

    def apply(h, w, i, between=None):
        t = nn(jnp.concatenate(split(w), axis=0), u_v[i])
        if between:
            between()
        t = nt(jnp.concatenate(split(t[:kh] + t[kh:]), axis=0), pick_v[i])
        return w + (t[:kh] + t[kh:])

    def project(i):
        mh, ml = split(m_v[pl.ds(i * step, step), :])
        t = nn(jnp.concatenate([mh, ml], axis=0), rh_v[...])
        zh, zl = split(t[:step] + t[step:] + nn(mh, rl_v[...]))
        zh_v[pl.ds(i * step, step), :] = zh
        zl_v[pl.ds(i * step, step), :] = zl

    def finish(h, wh, wl):
        t = nn(jnp.concatenate([wh, wl], axis=0), zh_v[...])
        g = t[:kh] + t[kh:] + nn(wh, zl_v[...])
        for c in range(cols):
            g_v[h, c] = g[:, c * width:(c + 1) * width].reshape(groups, rows, width)

    def first(k, i):
        h, c = chunks[k]
        return pltpu.make_async_remote_copy(
            g_v.at[h, c, partner(i)], spread[k].at[grp], s1.at[0], r1.at[k],
            device_id=group_peer(i), device_id_type=MESH)

    def second(k, i):
        h, c = chunks[k]
        return pltpu.make_async_remote_copy(
            arranged.at[h, c, partner(i)], seen.at[blk, h, c, grp], s2.at[0], r2.at[k],
            device_id=group_peer(i), device_id_type=MESH)

    def third(k, j):
        h, c = chunks[k]
        return pltpu.make_async_remote_copy(
            seen.at[blk, h, c], seen.at[blk, h, c], s3.at[0], r3.at[j, k],
            device_id=block_peer(j), device_id_type=MESH)

    def across(k, i, j):
        h, c = chunks[k]
        return pltpu.make_async_remote_copy(
            arranged.at[h, c, partner(i)], seen.at[blk, h, c, grp], s3.at[0], r3.at[j, k],
            device_id={"grp": partner(i), "blk": lax.rem(blk + j, blocks)}, device_id_type=MESH)

    def pieces(k, recv, send):
        h, c = chunks[k]
        return pltpu.make_async_remote_copy(
            arranged.at[h, c, pl.ds(0, groups - 1)], spread[k].at[pl.ds(0, groups - 1)], send, recv,
            device_id=block_peer(1), device_id_type=MESH)

    direct = (2, 3)

    copy_l.wait()
    copy_u[number - 1].wait()
    copy_r.wait()
    copy_m[0].wait()
    w = apply(0, jnp.transpose(l_v[:, :kh]), number - 1)
    rh_v[...], rl_v[...] = split(r_v[...])
    for i in range(parts):
        if i == 1:
            for c in copy_m[1:] + copy_u[:number - 1]:
                c.wait()
        u = number - 1 - i
        if i == 0:
            project(0)
        else:
            w = apply(0, w, u, functools.partial(project, i))
    finish(0, *split(w))

    pl.semaphore_wait(barrier, groups + blocks - 2)

    for k, (h, c) in enumerate(chunks):
        if h > 0 and c == 0:
            w = jnp.transpose(l_v[:, h * kh:(h + 1) * kh])
            for i in reversed(range(number)):
                w = apply(h, w, i)
            finish(h, *split(w))
        for i in pairs:
            first(k, i).start()
        spread[k][grp] = g_v[h, c, grp]

    for c in small:
        c.wait()
    targets = [target_ref[0, w] for w in range(groups)]
    for a in range(groups):
        found = 0
        for w in range(groups):
            found = jnp.where(targets[w] == a, w, found)
        source[a] = found

    momenta = sum_ref.shape[0]
    nw = kw // momenta
    sub = lax.broadcasted_iota(jnp.int32, (nw, kw), 0)
    lane = lax.broadcasted_iota(jnp.int32, (nw, kw), 1)
    for j in range(slots):
        t = own_ref[j]
        q = mom_ref[t]
        moved = sub + freq_ref[t]
        base = lane - jnp.where(moved >= nw, moved - nw, moved)
        for kappa in range(momenta):
            hit = jnp.where(base == sum_ref[kappa, q] * nw, 1.0, 0.0).astype(BF16)
            perm_v[j * kw + kappa * nw:j * kw + (kappa + 1) * nw, :] = hit

    for k, (h, c) in enumerate(chunks):
        pieces(k, r1.at[k], s1.at[0]).wait_recv()
        for i in pairs:
            a = partner(i)
            arranged[h, c, a] = spread[k][source[a]]
            second(k, i).start()
            if k in direct:
                for j in range(1, blocks):
                    across(k, i, j).start()
        mine = spread[k][source[grp]]
        seen[blk, h, c, grp] = mine
        if k in direct:
            arranged[h, c, grp] = mine
            for j in range(1, blocks):
                across(k, 0, j).start()

    def other(j):
        return lax.rem(blk + blocks - j, blocks)

    for k in range(len(chunks)):
        if k not in direct:
            pieces(k, r2.at[k], s2.at[0]).wait_recv()
            for j in range(1, blocks):
                third(k, j).start()

    copy_p.wait()
    for h in range(halves):
        now = [k for k in range(len(chunks)) if chunks[k][0] == h]
        for k in now:
            if k in direct:
                pieces(k, r2.at[k], s2.at[0]).wait_recv()
        accumulate(blk, h)
        for j in range(1, blocks):
            for k in now:
                third(k, j).wait_recv()
            accumulate(other(j), h)

    for k in range(len(chunks)):
        pieces(k, r1.at[k], s1.at[0]).wait_send()
        pieces(k, r2.at[k], s2.at[0]).wait_send()
        for j in range(1, blocks):
            third(k, j).wait_send()


def shards(
    walker_matrix,
    updates,
    update_rows,
    left_table,
    right_table,
    assignment,
    momentum_sum,
    transfer_momentum,
    transfer_frequency,
    ownership,
    g4_prior,
):
    groups = lax.axis_size("grp")
    blocks = lax.axis_size("blk")
    order, kw = left_table.shape
    number, rank = updates.shape[2], updates.shape[4]
    hbm = pl.BlockSpec(memory_space=pltpu.HBM)
    halves = 2 if kw // groups % 16 == 0 else 1
    cols = 2 if kw % 256 == 0 else 1
    rows, width = kw // groups // halves, kw // cols
    slots = g4_prior.shape[1]
    room = 4 * slots * kw * kw
    summed = pl.pallas_call(
        functools.partial(exchange_kernel, groups, blocks),
        out_shape=pltpu.VMEM((slots, kw, kw), F32),
        in_specs=[hbm] * 11,
        out_specs=pl.BlockSpec(memory_space=pltpu.VMEM),
        scratch_shapes=[
            pltpu.SMEM(assignment.shape, jnp.int32),
            pltpu.SMEM(ownership.shape, jnp.int32),
            pltpu.SMEM(transfer_momentum.shape, jnp.int32),
            pltpu.SMEM(transfer_frequency.shape, jnp.int32),
            pltpu.SMEM(momentum_sum.shape, jnp.int32),
            pltpu.VMEM((order, order), F32),
            pltpu.VMEM((number, order, rank), BF16),
            pltpu.VMEM((number, rank), jnp.int32),
            pltpu.VMEM((order, kw), F32),
            pltpu.VMEM((order, kw), F32),
            pltpu.VMEM((number, order, rank), BF16),
            pltpu.VMEM((order, kw), BF16),
            pltpu.VMEM((order, kw), BF16),
            pltpu.VMEM((order, kw), BF16),
            pltpu.VMEM((order, kw), BF16),
            pltpu.VMEM((halves, cols, groups, rows, width), F32),
            pltpu.VMEM((halves, cols, groups, rows, width), F32),
            pltpu.VMEM((blocks, halves, cols, groups, rows, width), F32),
            pltpu.VMEM((slots * kw, kw), BF16),
            pltpu.VMEM((blocks, slots, kw, kw), F32),
            pltpu.SMEM((groups,), jnp.int32),
            pltpu.SemaphoreType.DMA((number + 13,)),
            pltpu.SemaphoreType.DMA((1,)),
            pltpu.SemaphoreType.DMA((halves * cols,)),
            pltpu.SemaphoreType.DMA((1,)),
            pltpu.SemaphoreType.DMA((halves * cols,)),
            pltpu.SemaphoreType.DMA((1,)),
            pltpu.SemaphoreType.DMA((blocks, halves * cols)),
        ] + [pltpu.VMEM((groups, rows, width), F32)] * (halves * cols),
        compiler_params=pltpu.CompilerParams(
            collective_id=0, has_side_effects=True, vmem_limit_bytes=67043328 - room),
        name="exchange",
    )(assignment, ownership, transfer_momentum, transfer_frequency, momentum_sum,
      walker_matrix[0, 0], updates[0, 0], update_rows[0, 0], left_table, right_table, g4_prior[0])
    return summed[None]


def solution(mesh):
    placed = (
        P("grp", "blk", None, None),
        P("grp", "blk", None, None, None),
        P("grp", "blk", None, None),
        P(),
        P(),
        P("blk", None),
        P(),
        P(),
        P(),
        P("blk"),
        P("grp", "blk", None, None),
    )
    return jax.shard_map(
        shards, mesh=mesh, in_specs=placed, out_specs=P("grp", "blk", None, None), check_vma=False
    )
```

```python
import functools

import jax
import jax.numpy as jnp
from jax import lax
from jax.experimental import pallas as pl
from jax.experimental.pallas import tpu as pltpu
from jax.sharding import PartitionSpec as P

MESH = pl.DeviceIdType.MESH
F32 = jnp.float32
BF16 = jnp.bfloat16


def split(x):
    hi = x.astype(BF16)
    return hi, (x - hi.astype(F32)).astype(BF16)


def nn(a, b):
    return jnp.dot(a, b, preferred_element_type=F32)


def nt(a, b):
    return lax.dot_general(a, b, (((1,), (1,)), ((), ())), preferred_element_type=F32)


def exchange_kernel(
    groups, blocks, target_hbm, own_hbm, mom_hbm, freq_hbm, sum_hbm, m_hbm, u_hbm, rows_hbm, l_hbm, r_hbm, prior_hbm, out_ref,
    target_ref, own_ref, mom_ref, freq_ref, sum_ref, m_v, u_v, rows_v, l_v, r_v, pick_v, rh_v, rl_v, zh_v, zl_v, g_v, arranged, seen, perm_v, part_v, source,
    sems, s1, r1, s2, r2, s3, r3, *spread,
):
    grp = lax.axis_index("grp")
    blk = lax.axis_index("blk")
    number, order, rank = u_v.shape
    halves, cols, _, rows, width = g_v.shape
    kw = cols * width
    kh = kw // halves
    parts = 4
    step = order // parts
    slots = out_ref.shape[0]
    chunks = [(h, c) for h in range(halves) for c in range(cols)]
    pairs = list(range(1, groups))
    hold = g_v.shape[2]
    edge = (groups - hold) // 2
    me = lax.rem(grp - edge + groups, hold)
    holder = (grp >= edge) & (grp < edge + hold)
    outside = jnp.logical_not(holder)

    def flip(start, i):
        place, bit = start, 1
        while bit <= i:
            if i & bit:
                place = place + bit - 2 * bit * lax.rem(start // bit, 2)
            bit *= 2
        return place

    def partner(i):
        return flip(grp, i)

    def group_peer(i):
        return {"grp": partner(i), "blk": blk}

    def block_peer(i):
        return {"grp": grp, "blk": lax.rem(blk + i, blocks)}

    copy_rows = pltpu.make_async_copy(rows_hbm, rows_v, sems.at[0])
    copy_l = pltpu.make_async_copy(l_hbm, l_v, sems.at[1])
    copy_r = pltpu.make_async_copy(r_hbm, r_v, sems.at[2])
    copy_p = pltpu.make_async_copy(prior_hbm, out_ref, sems.at[3])
    copy_u = [pltpu.make_async_copy(u_hbm.at[i], u_v.at[i], sems.at[4 + i]) for i in range(number)]
    copy_m = [
        pltpu.make_async_copy(m_hbm.at[pl.ds(i * step, step)], m_v.at[pl.ds(i * step, step)], sems.at[4 + number + i])
        for i in range(parts)
    ]
    copy_rows.start()
    copy_l.start()
    copy_u[number - 1].start()
    copy_r.start()
    copy_m[0].start()
    later = [copy_u[number - 2], copy_m[1], copy_u[number - 3], copy_m[2], copy_u[number - 4], copy_m[3], copy_p]
    for c in later:
        c.start()

    small = [(target_hbm, target_ref), (own_hbm, own_ref), (mom_hbm, mom_ref), (freq_hbm, freq_ref), (sum_hbm, sum_ref)]
    small = [pltpu.make_async_copy(a, b, sems.at[4 + number + parts + i]) for i, (a, b) in enumerate(small)]
    for c in small:
        c.start()

    barrier = pltpu.get_barrier_semaphore()

    for i in pairs:
        pl.semaphore_signal(barrier, inc=1, device_id=group_peer(i), device_id_type=MESH)

    @pl.loop(1, blocks)
    def _(i):
        pl.semaphore_signal(barrier, inc=1, device_id=block_peer(i), device_id_type=MESH)

    copy_rows.wait()
    for i in reversed(range(number)):
        pick_v[i] = jnp.where(
            lax.broadcasted_iota(jnp.int32, (order, rank), 0) == rows_v[pl.ds(i, 1), :], 1.0, 0.0
        ).astype(BF16)

    def rows_of(b, h):
        return jnp.concatenate([seen[b, h, c].reshape(kh, width) for c in range(cols)], axis=1)

    def accumulate(b, h):
        x = nt(perm_v[...], jnp.concatenate(split(rows_of(b, h)), axis=0)).astype(BF16)
        last = h == halves - 1
        if last:
            g = jnp.concatenate([rows_of(b, i) for i in range(halves)], axis=0)
        for j in range(slots):
            here = slice(j * kw, (j + 1) * kw)
            p = perm_v[here, h * kh:(h + 1) * kh]
            y = nt(x[here], jnp.concatenate([p, p], axis=1))
            if h > 0:
                y = y + part_v[b, j]
            if last:
                out_ref[j] = out_ref[j] + g * y * (1.0 / blocks)
            else:
                part_v[b, j] = y

    def apply(h, w, i, between=None):
        t = nn(jnp.concatenate(split(w), axis=0), u_v[i])
        if between:
            between()
        t = nt(jnp.concatenate(split(t[:kh] + t[kh:]), axis=0), pick_v[i])
        return w + (t[:kh] + t[kh:])

    def project(i):
        mh, ml = split(m_v[pl.ds(i * step, step), :])
        t = nn(jnp.concatenate([mh, ml], axis=0), rh_v[...])
        zh, zl = split(t[:step] + t[step:] + nn(mh, rl_v[...]))
        zh_v[pl.ds(i * step, step), :] = zh
        zl_v[pl.ds(i * step, step), :] = zl

    def finish(h, wh, wl):
        t = nn(jnp.concatenate([wh, wl], axis=0), zh_v[...])
        g = t[:kh] + t[kh:] + nn(wh, zl_v[...])
        for c in range(cols):
            g_v[h, c] = g[:, c * width:(c + 1) * width].reshape(hold, rows, width)

    def first(k, i):
        h, c = chunks[k]
        q = flip(me, i)
        return pltpu.make_async_remote_copy(
            g_v.at[h, c, q], spread[k].at[grp], s1.at[0], r1.at[k],
            device_id={"grp": q + edge, "blk": blk}, device_id_type=MESH)

    def second(k, i):
        h, c = chunks[k]
        return pltpu.make_async_remote_copy(
            arranged.at[h, c, partner(i)], seen.at[blk, h, c, me], s2.at[0], r2.at[k],
            device_id=group_peer(i), device_id_type=MESH)

    def third(k, j):
        h, c = chunks[k]
        return pltpu.make_async_remote_copy(
            seen.at[blk, h, c], seen.at[blk, h, c], s3.at[0], r3.at[j, k],
            device_id=block_peer(j), device_id_type=MESH)

    def across(k, i, j):
        h, c = chunks[k]
        return pltpu.make_async_remote_copy(
            arranged.at[h, c, partner(i)], seen.at[blk, h, c, me], s3.at[0], r3.at[j, k],
            device_id={"grp": partner(i), "blk": lax.rem(blk + j, blocks)}, device_id_type=MESH)

    def bytes_of(count, recv, send):
        return pltpu.make_async_remote_copy(
            arranged.at[0, 0, pl.ds(0, count)], arranged.at[0, 0, pl.ds(0, count)], send, recv,
            device_id=block_peer(1), device_id_type=MESH)

    direct = [len(chunks) - 1]

    def arrived(k):
        @pl.when(holder)
        def _():
            bytes_of(hold - 1, r2.at[k], s2.at[0]).wait_recv()

        @pl.when(outside)
        def _():
            bytes_of(hold, r2.at[k], s2.at[0]).wait_recv()

    copy_l.wait()
    copy_u[number - 1].wait()
    copy_r.wait()
    copy_m[0].wait()
    w = apply(0, jnp.transpose(l_v[:, :kh]), number - 1)
    rh_v[...], rl_v[...] = split(r_v[...])
    for i in range(parts):
        if i == 1:
            for c in copy_m[1:] + copy_u[:number - 1]:
                c.wait()
        u = number - 1 - i
        if i == 0:
            project(0)
        else:
            w = apply(0, w, u, functools.partial(project, i))
    finish(0, *split(w))

    pl.semaphore_wait(barrier, groups + blocks - 2)

    for k, (h, c) in enumerate(chunks):
        if h > 0 and c == 0:
            w = jnp.transpose(l_v[:, h * kh:(h + 1) * kh])
            for i in reversed(range(number)):
                w = apply(h, w, i)
            finish(h, *split(w))
        for i in range(1, hold):
            first(k, i).start()

        @pl.when(outside)
        def _():
            first(k, 0).start()

        @pl.when(holder)
        def _():
            spread[k][grp] = g_v[h, c, me]

    for c in small:
        c.wait()
    targets = [target_ref[0, w] for w in range(groups)]
    for a in range(groups):
        found = 0
        for w in range(groups):
            found = jnp.where(targets[w] == a, w, found)
        source[a] = found

    momenta = sum_ref.shape[0]
    nw = kw // momenta
    sub = lax.broadcasted_iota(jnp.int32, (nw, kw), 0)
    lane = lax.broadcasted_iota(jnp.int32, (nw, kw), 1)
    for j in range(slots):
        t = own_ref[j]
        q = mom_ref[t]
        moved = sub + freq_ref[t]
        base = lane - jnp.where(moved >= nw, moved - nw, moved)
        for kappa in range(momenta):
            hit = jnp.where(base == sum_ref[kappa, q] * nw, 1.0, 0.0).astype(BF16)
            perm_v[j * kw + kappa * nw:j * kw + (kappa + 1) * nw, :] = hit

    @pl.when(holder)
    def _():
        for k, (h, c) in enumerate(chunks):
            bytes_of(groups - 1, r1.at[k], s1.at[0]).wait_recv()
            for i in pairs:
                a = partner(i)
                arranged[h, c, a] = spread[k][source[a]]
                second(k, i).start()
                if k in direct:
                    for j in range(1, blocks):
                        across(k, i, j).start()
            mine = spread[k][source[grp]]
            seen[blk, h, c, me] = mine
            if k in direct:
                arranged[h, c, grp] = mine
                for j in range(1, blocks):
                    across(k, 0, j).start()

    def other(j):
        return lax.rem(blk + blocks - j, blocks)

    for k in range(len(chunks)):
        if k not in direct:
            arrived(k)
            for j in range(1, blocks):
                third(k, j).start()

    copy_p.wait()
    for h in range(halves):
        now = [k for k in range(len(chunks)) if chunks[k][0] == h]
        for k in now:
            if k in direct:
                arrived(k)
        accumulate(blk, h)
        for j in range(1, blocks):
            for k in now:
                third(k, j).wait_recv()
            accumulate(other(j), h)

    for k in range(len(chunks)):
        bytes_of(hold - 1, r1.at[k], s1.at[0]).wait_send()
        if k not in direct:
            for j in range(1, blocks):
                third(k, j).wait_send()

    @pl.when(outside)
    def _():
        for k in range(len(chunks)):
            bytes_of(1, r1.at[k], s1.at[0]).wait_send()

    @pl.when(holder)
    def _():
        for k in range(len(chunks)):
            bytes_of(groups - 1, r2.at[k], s2.at[0]).wait_send()
            if k in direct:
                for j in range(1, blocks):
                    bytes_of(groups, r2.at[k], s3.at[0]).wait_send()


def shards(
    walker_matrix,
    updates,
    update_rows,
    left_table,
    right_table,
    assignment,
    momentum_sum,
    transfer_momentum,
    transfer_frequency,
    ownership,
    g4_prior,
):
    groups = lax.axis_size("grp")
    blocks = lax.axis_size("blk")
    order, kw = left_table.shape
    number, rank = updates.shape[2], updates.shape[4]
    hbm = pl.BlockSpec(memory_space=pltpu.HBM)
    hold = groups // 2 if groups % 4 == 0 else groups
    halves = 2 if kw // hold % 16 == 0 else 1
    cols = 2 if kw % 256 == 0 else 1
    rows, width = kw // hold // halves, kw // cols
    slots = g4_prior.shape[1]
    room = 4 * slots * kw * kw
    summed = pl.pallas_call(
        functools.partial(exchange_kernel, groups, blocks),
        out_shape=pltpu.VMEM((slots, kw, kw), F32),
        in_specs=[hbm] * 11,
        out_specs=pl.BlockSpec(memory_space=pltpu.VMEM),
        scratch_shapes=[
            pltpu.SMEM(assignment.shape, jnp.int32),
            pltpu.SMEM(ownership.shape, jnp.int32),
            pltpu.SMEM(transfer_momentum.shape, jnp.int32),
            pltpu.SMEM(transfer_frequency.shape, jnp.int32),
            pltpu.SMEM(momentum_sum.shape, jnp.int32),
            pltpu.VMEM((order, order), F32),
            pltpu.VMEM((number, order, rank), BF16),
            pltpu.VMEM((number, rank), jnp.int32),
            pltpu.VMEM((order, kw), F32),
            pltpu.VMEM((order, kw), F32),
            pltpu.VMEM((number, order, rank), BF16),
            pltpu.VMEM((order, kw), BF16),
            pltpu.VMEM((order, kw), BF16),
            pltpu.VMEM((order, kw), BF16),
            pltpu.VMEM((order, kw), BF16),
            pltpu.VMEM((halves, cols, hold, rows, width), F32),
            pltpu.VMEM((halves, cols, groups, rows, width), F32),
            pltpu.VMEM((blocks, halves, cols, hold, rows, width), F32),
            pltpu.VMEM((slots * kw, kw), BF16),
            pltpu.VMEM((blocks, slots, kw, kw), F32),
            pltpu.SMEM((groups,), jnp.int32),
            pltpu.SemaphoreType.DMA((number + 13,)),
            pltpu.SemaphoreType.DMA((1,)),
            pltpu.SemaphoreType.DMA((halves * cols,)),
            pltpu.SemaphoreType.DMA((1,)),
            pltpu.SemaphoreType.DMA((halves * cols,)),
            pltpu.SemaphoreType.DMA((1,)),
            pltpu.SemaphoreType.DMA((blocks, halves * cols)),
        ] + [pltpu.VMEM((groups, rows, width), F32)] * (halves * cols),
        compiler_params=pltpu.CompilerParams(
            collective_id=0, has_side_effects=True, vmem_limit_bytes=67043328 - room),
        name="exchange",
    )(assignment, ownership, transfer_momentum, transfer_frequency, momentum_sum,
      walker_matrix[0, 0], updates[0, 0], update_rows[0, 0], left_table, right_table, g4_prior[0])
    return summed[None]


def solution(mesh):
    placed = (
        P("grp", "blk", None, None),
        P("grp", "blk", None, None, None),
        P("grp", "blk", None, None),
        P(),
        P(),
        P("blk", None),
        P(),
        P(),
        P(),
        P("blk"),
        P("grp", "blk", None, None),
    )
    return jax.shard_map(
        shards, mesh=mesh, in_specs=placed, out_specs=P("grp", "blk", None, None), check_vma=False
    )
```

```python
import functools

import jax
import jax.numpy as jnp
from jax import lax
from jax.experimental import pallas as pl
from jax.experimental.pallas import tpu as pltpu
from jax.sharding import PartitionSpec as P

MESH = pl.DeviceIdType.MESH
F32 = jnp.float32
BF16 = jnp.bfloat16


def split(x):
    hi = x.astype(BF16)
    return hi, (x - hi.astype(F32)).astype(BF16)


def nn(a, b):
    return jnp.dot(a, b, preferred_element_type=F32)


def nt(a, b):
    return lax.dot_general(a, b, (((1,), (1,)), ((), ())), preferred_element_type=F32)


def exchange_kernel(
    groups, blocks, target_hbm, own_hbm, mom_hbm, freq_hbm, sum_hbm, m_hbm, u_hbm, rows_hbm, l_hbm, r_hbm, prior_hbm, out_ref,
    target_ref, own_ref, mom_ref, freq_ref, sum_ref, m_v, u_v, rows_v, l_v, r_v, pick_v, rh_v, rl_v, zh_v, zl_v, g_v, arranged, seen, perm_v, part_v, source,
    sems, s1, r1, s2, r2, s3, r3, *spread,
):
    grp = lax.axis_index("grp")
    blk = lax.axis_index("blk")
    number, order, rank = u_v.shape
    halves, cols, _, rows, width = g_v.shape
    kw = cols * width
    kh = kw // halves
    parts = 4
    step = order // parts
    slots = out_ref.shape[0]
    chunks = [(h, c) for h in range(halves) for c in range(cols)]
    pairs = list(range(1, groups))
    hold = g_v.shape[2]
    edge = (groups - hold) // 2
    me = lax.rem(grp - edge + groups, hold)
    holder = (grp >= edge) & (grp < edge + hold)
    outside = jnp.logical_not(holder)

    def flip(start, i):
        place, bit = start, 1
        while bit <= i:
            if i & bit:
                place = place + bit - 2 * bit * lax.rem(start // bit, 2)
            bit *= 2
        return place

    def partner(i):
        return flip(grp, i)

    def group_peer(i):
        return {"grp": partner(i), "blk": blk}

    def block_peer(i):
        return {"grp": grp, "blk": lax.rem(blk + i, blocks)}

    copy_rows = pltpu.make_async_copy(rows_hbm, rows_v, sems.at[0])
    copy_l = pltpu.make_async_copy(l_hbm, l_v, sems.at[1])
    copy_r = pltpu.make_async_copy(r_hbm, r_v, sems.at[2])
    copy_p = pltpu.make_async_copy(prior_hbm, out_ref, sems.at[3])
    copy_u = [pltpu.make_async_copy(u_hbm.at[i], u_v.at[i], sems.at[4 + i]) for i in range(number)]
    copy_m = [
        pltpu.make_async_copy(m_hbm.at[pl.ds(i * step, step)], m_v.at[pl.ds(i * step, step)], sems.at[4 + number + i])
        for i in range(parts)
    ]
    copy_rows.start()
    copy_l.start()
    copy_u[number - 1].start()
    copy_r.start()
    copy_m[0].start()
    later = [copy_u[number - 2], copy_m[1], copy_u[number - 3], copy_m[2], copy_u[number - 4], copy_m[3], copy_p]
    for c in later:
        c.start()

    small = [(target_hbm, target_ref), (own_hbm, own_ref), (mom_hbm, mom_ref), (freq_hbm, freq_ref), (sum_hbm, sum_ref)]
    small = [pltpu.make_async_copy(a, b, sems.at[4 + number + parts + i]) for i, (a, b) in enumerate(small)]
    for c in small:
        c.start()

    barrier = pltpu.get_barrier_semaphore()

    for i in pairs:
        pl.semaphore_signal(barrier, inc=1, device_id=group_peer(i), device_id_type=MESH)

    @pl.loop(1, blocks)
    def _(i):
        pl.semaphore_signal(barrier, inc=1, device_id=block_peer(i), device_id_type=MESH)

    copy_rows.wait()
    for i in reversed(range(number)):
        pick_v[i] = jnp.where(
            lax.broadcasted_iota(jnp.int32, (order, rank), 0) == rows_v[pl.ds(i, 1), :], 1.0, 0.0
        ).astype(BF16)

    def rows_of(b, h):
        return jnp.concatenate([seen[b, h, c].reshape(kh, width) for c in range(cols)], axis=1)

    def accumulate(b, h):
        x = nt(perm_v[...], jnp.concatenate(split(rows_of(b, h)), axis=0)).astype(BF16)
        last = h == halves - 1
        if last:
            g = jnp.concatenate([rows_of(b, i) for i in range(halves)], axis=0)
        for j in range(slots):
            here = slice(j * kw, (j + 1) * kw)
            p = perm_v[here, h * kh:(h + 1) * kh]
            y = nt(x[here], jnp.concatenate([p, p], axis=1))
            if h > 0:
                y = y + part_v[b, j]
            if last:
                out_ref[j] = out_ref[j] + g * y * (1.0 / blocks)
            else:
                part_v[b, j] = y

    def apply(h, w, i, between=None):
        t = nn(jnp.concatenate(split(w), axis=0), u_v[i])
        if between:
            between()
        t = nt(jnp.concatenate(split(t[:kh] + t[kh:]), axis=0), pick_v[i])
        return w + (t[:kh] + t[kh:])

    def project(i):
        mh, ml = split(m_v[pl.ds(i * step, step), :])
        t = nn(jnp.concatenate([mh, ml], axis=0), rh_v[...])
        zh, zl = split(t[:step] + t[step:] + nn(mh, rl_v[...]))
        zh_v[pl.ds(i * step, step), :] = zh
        zl_v[pl.ds(i * step, step), :] = zl

    def finish(h, wh, wl):
        t = nn(jnp.concatenate([wh, wl], axis=0), zh_v[...])
        g = t[:kh] + t[kh:] + nn(wh, zl_v[...])
        for c in range(cols):
            g_v[h, c] = g[:, c * width:(c + 1) * width].reshape(hold, rows, width)

    def first(k, i):
        h, c = chunks[k]
        q = flip(me, i)
        return pltpu.make_async_remote_copy(
            g_v.at[h, c, q], spread[k].at[grp], s1.at[0], r1.at[k],
            device_id={"grp": q + edge, "blk": blk}, device_id_type=MESH)

    def second(k, i):
        h, c = chunks[k]
        return pltpu.make_async_remote_copy(
            arranged.at[h, c, partner(i)], seen.at[blk, h, c, me], s2.at[0], r2.at[k],
            device_id=group_peer(i), device_id_type=MESH)

    def third(k, j):
        h, c = chunks[k]
        return pltpu.make_async_remote_copy(
            seen.at[blk, h, c], seen.at[blk, h, c], s3.at[0], r3.at[j, k],
            device_id=block_peer(j), device_id_type=MESH)

    def across(k, i, j):
        h, c = chunks[k]
        return pltpu.make_async_remote_copy(
            arranged.at[h, c, partner(i)], seen.at[blk, h, c, me], s3.at[0], r3.at[j, k],
            device_id={"grp": partner(i), "blk": lax.rem(blk + j, blocks)}, device_id_type=MESH)

    def bytes_of(count, recv, send):
        return pltpu.make_async_remote_copy(
            arranged.at[0, 0, pl.ds(0, count)], arranged.at[0, 0, pl.ds(0, count)], send, recv,
            device_id=block_peer(1), device_id_type=MESH)

    direct = [len(chunks) - 1]

    def arrived(k):
        @pl.when(holder)
        def _():
            bytes_of(hold - 1, r2.at[k], s2.at[0]).wait_recv()

        @pl.when(outside)
        def _():
            bytes_of(hold, r2.at[k], s2.at[0]).wait_recv()

    copy_l.wait()
    copy_u[number - 1].wait()
    copy_r.wait()
    copy_m[0].wait()
    w = apply(0, jnp.transpose(l_v[:, :kh]), number - 1)
    rh_v[...], rl_v[...] = split(r_v[...])
    for i in range(parts):
        if i == 1:
            for c in copy_m[1:] + copy_u[:number - 1]:
                c.wait()
        u = number - 1 - i
        if i == 0:
            project(0)
        else:
            w = apply(0, w, u, functools.partial(project, i))
    finish(0, *split(w))

    pl.semaphore_wait(barrier, groups + blocks - 2)

    for k, (h, c) in enumerate(chunks):
        if h > 0 and c == 0:
            w = jnp.transpose(l_v[:, h * kh:(h + 1) * kh])
            for i in reversed(range(number)):
                w = apply(h, w, i)
            finish(h, *split(w))
        for i in range(1, hold):
            first(k, i).start()

        @pl.when(outside)
        def _():
            first(k, 0).start()

        @pl.when(holder)
        def _():
            spread[k][grp] = g_v[h, c, me]

    for c in small:
        c.wait()
    targets = [target_ref[0, w] for w in range(groups)]
    for a in range(groups):
        found = 0
        for w in range(groups):
            found = jnp.where(targets[w] == a, w, found)
        source[a] = found

    momenta = sum_ref.shape[0]
    nw = kw // momenta
    sub = lax.broadcasted_iota(jnp.int32, (nw, kw), 0)
    lane = lax.broadcasted_iota(jnp.int32, (nw, kw), 1)
    for j in range(slots):
        t = own_ref[j]
        q = mom_ref[t]
        moved = sub + freq_ref[t]
        base = lane - jnp.where(moved >= nw, moved - nw, moved)
        for kappa in range(momenta):
            hit = jnp.where(base == sum_ref[kappa, q] * nw, 1.0, 0.0).astype(BF16)
            perm_v[j * kw + kappa * nw:j * kw + (kappa + 1) * nw, :] = hit

    @pl.when(holder)
    def _():
        for k, (h, c) in enumerate(chunks):
            bytes_of(groups - 1, r1.at[k], s1.at[0]).wait_recv()
            for i in pairs:
                a = partner(i)
                arranged[h, c, a] = spread[k][source[a]]
                if k in direct:
                    for j in range(1, blocks):
                        across(k, i, j).start()
                second(k, i).start()
            mine = spread[k][source[grp]]
            seen[blk, h, c, me] = mine
            if k in direct:
                arranged[h, c, grp] = mine
                for j in range(1, blocks):
                    across(k, 0, j).start()

    def other(j):
        return lax.rem(blk + blocks - j, blocks)

    for k in range(len(chunks)):
        if k not in direct:
            arrived(k)
            for j in range(1, blocks):
                third(k, j).start()

    copy_p.wait()
    for h in range(halves):
        now = [k for k in range(len(chunks)) if chunks[k][0] == h]
        for k in now:
            if k in direct:
                arrived(k)
        accumulate(blk, h)
        for j in range(1, blocks):
            for k in now:
                third(k, j).wait_recv()
            accumulate(other(j), h)

    for k in range(len(chunks)):
        bytes_of(hold - 1, r1.at[k], s1.at[0]).wait_send()
        if k not in direct:
            for j in range(1, blocks):
                third(k, j).wait_send()

    @pl.when(outside)
    def _():
        for k in range(len(chunks)):
            bytes_of(1, r1.at[k], s1.at[0]).wait_send()

    @pl.when(holder)
    def _():
        for k in range(len(chunks)):
            bytes_of(groups - 1, r2.at[k], s2.at[0]).wait_send()
            if k in direct:
                for j in range(1, blocks):
                    bytes_of(groups, r2.at[k], s3.at[0]).wait_send()


def shards(
    walker_matrix,
    updates,
    update_rows,
    left_table,
    right_table,
    assignment,
    momentum_sum,
    transfer_momentum,
    transfer_frequency,
    ownership,
    g4_prior,
):
    groups = lax.axis_size("grp")
    blocks = lax.axis_size("blk")
    order, kw = left_table.shape
    number, rank = updates.shape[2], updates.shape[4]
    hbm = pl.BlockSpec(memory_space=pltpu.HBM)
    hold = groups // 2 if groups % 4 == 0 else groups
    halves = 2 if kw // hold % 16 == 0 else 1
    cols = 2 if kw % 256 == 0 else 1
    rows, width = kw // hold // halves, kw // cols
    slots = g4_prior.shape[1]
    room = 4 * slots * kw * kw
    summed = pl.pallas_call(
        functools.partial(exchange_kernel, groups, blocks),
        out_shape=pltpu.VMEM((slots, kw, kw), F32),
        in_specs=[hbm] * 11,
        out_specs=pl.BlockSpec(memory_space=pltpu.VMEM),
        scratch_shapes=[
            pltpu.SMEM(assignment.shape, jnp.int32),
            pltpu.SMEM(ownership.shape, jnp.int32),
            pltpu.SMEM(transfer_momentum.shape, jnp.int32),
            pltpu.SMEM(transfer_frequency.shape, jnp.int32),
            pltpu.SMEM(momentum_sum.shape, jnp.int32),
            pltpu.VMEM((order, order), F32),
            pltpu.VMEM((number, order, rank), BF16),
            pltpu.VMEM((number, rank), jnp.int32),
            pltpu.VMEM((order, kw), F32),
            pltpu.VMEM((order, kw), F32),
            pltpu.VMEM((number, order, rank), BF16),
            pltpu.VMEM((order, kw), BF16),
            pltpu.VMEM((order, kw), BF16),
            pltpu.VMEM((order, kw), BF16),
            pltpu.VMEM((order, kw), BF16),
            pltpu.VMEM((halves, cols, hold, rows, width), F32),
            pltpu.VMEM((halves, cols, groups, rows, width), F32),
            pltpu.VMEM((blocks, halves, cols, hold, rows, width), F32),
            pltpu.VMEM((slots * kw, kw), BF16),
            pltpu.VMEM((blocks, slots, kw, kw), F32),
            pltpu.SMEM((groups,), jnp.int32),
            pltpu.SemaphoreType.DMA((number + 13,)),
            pltpu.SemaphoreType.DMA((1,)),
            pltpu.SemaphoreType.DMA((halves * cols,)),
            pltpu.SemaphoreType.DMA((1,)),
            pltpu.SemaphoreType.DMA((halves * cols,)),
            pltpu.SemaphoreType.DMA((1,)),
            pltpu.SemaphoreType.DMA((blocks, halves * cols)),
        ] + [pltpu.VMEM((groups, rows, width), F32)] * (halves * cols),
        compiler_params=pltpu.CompilerParams(
            collective_id=0, has_side_effects=True, vmem_limit_bytes=67043328 - room),
        name="exchange",
    )(assignment, ownership, transfer_momentum, transfer_frequency, momentum_sum,
      walker_matrix[0, 0], updates[0, 0], update_rows[0, 0], left_table, right_table, g4_prior[0])
    return summed[None]


def solution(mesh):
    placed = (
        P("grp", "blk", None, None),
        P("grp", "blk", None, None, None),
        P("grp", "blk", None, None),
        P(),
        P(),
        P("blk", None),
        P(),
        P(),
        P(),
        P("blk"),
        P("grp", "blk", None, None),
    )
    return jax.shard_map(
        shards, mesh=mesh, in_specs=placed, out_specs=P("grp", "blk", None, None), check_vma=False
    )
```
